256 devices in a mesh: chan: 128 (over x_lo, z, y, core), tm: 2 (over x_hi).
Axes of the slice: x: 4 (x_hi: 2, x_lo: 2; x = x_hi * 2 + x_lo), y: 4, z: 8, core: 2. Of those that a mesh axis runs over, the one named last changes fastest.
Arguments:
- records: bfloat16 [6, 2048, 16384], P('tm', None, 'chan'), may hold values from -600 to 600
- band_taps: float32 [64], replicated, may hold values from -0.75 to 0.75
- white_taps: float32 [16, 16384], P(None, 'chan'), may hold values from -1.5 to 1.5
- live_mask: int32 [16384], P('chan'), may hold values 0 or 1
- partners: int32 [6, 128], P(None, 'chan'), may hold values from 0 to 127, as said below
Outputs:
- correlations: float32 [6, 32, 16384, 128], P(None, 'tm', 'chan')
The draws below stay inside these ranges and needn't reach their ends.
Inputs may be any that keep to these rules, and one draw needn't show every extreme that they name: In each round blocks are matched in pairs: partners[r, b] differs from b, partners[r, partners[r, b]] = b, and partners[r, b] - b equals d or -d modulo 128, with the same d in the finite set (1, 2, 4) for all blocks of the round. Over all rounds every block b is matched with b + 1, b - 1, b + 2, b - 2, b + 4 and b - 4 modulo 128, each once.
All inputs are finite; a program needn't handle non-finite values. No bound on the sum of `live_mask` on one device may be relied on, other than what follows from the above.
Results may differ from the reference program's by a relative error of at most 0.0058.
Values may be sent and summed in bfloat16 or wider, within the bound.
No kernel may reach another device: no remote copies, remote signals or barrier semaphores. Data moves between devices by JAX's collectives and lax.ppermute only.
A program may use at most 64 MiB of HBM per device.

```python
import math
import jax
import jax.numpy as jnp
from jax import lax

CB = 128
SAMP = 2048
NB = 128
SEG = 6
BT = 64
WT = 16
ROUNDS = 6
LAGS = 32
BLOCKS = 128
CHANNELS = 16384


def draw_records(key, part):
    sub_keys = jax.random.split(key, 3)
    chan_scale = jnp.exp(jax.random.uniform(sub_keys[0], (1, 1, CHANNELS)) * math.log(10.0))
    seg_scale = jnp.exp(jax.random.uniform(sub_keys[1], (SEG, 1, CHANNELS)) * math.log(10.0))
    base_noise = jnp.clip(jax.random.normal(sub_keys[2], (SEG, SAMP, CHANNELS)), -6.0, 6.0)
    return (base_noise * chan_scale * seg_scale).astype(jnp.bfloat16)


def draw_partners(key, part):
    order = jax.random.permutation(jax.random.fold_in(key, 12), ROUNDS).astype(jnp.int32)
    distances = jnp.array([1, 1, 2, 2, 4, 4], dtype=jnp.int32)[order]
    phases = jnp.array([0, 1, 0, 1, 0, 1], dtype=jnp.int32)[order]
    block_ids = jnp.arange(BLOCKS, dtype=jnp.int32)[None, :]
    upward = jnp.mod(block_ids // distances[:, None], 2) == phases[:, None]
    mates = jnp.where(upward, block_ids + distances[:, None], block_ids - distances[:, None])
    return jnp.mod(mates, BLOCKS).astype(jnp.int32)


def plant(values, rng, smallest, top_value):
    extent = values.shape
    spot = [jax.random.randint(jax.random.fold_in(rng, axis), (), 0, extent[axis]) for axis in range(len(extent))]
    values = values.at[tuple(spot)].set(smallest)
    longest = extent.index(max(extent))
    spot[longest] = (spot[longest] + 1) % extent[longest]
    return values.at[tuple(spot)].set(top_value)


def block_levels(own_key, shape, pieces, low, top_value):
    loudness, own = 1.0, jax.random.fold_in(own_key, 6)
    for axis_at, shards_of in pieces:
        heights = jnp.exp(jax.random.uniform(jax.random.fold_in(own, axis_at), (shards_of,), jnp.float32, low / len(pieces), top_value / len(pieces)))
        loudness = loudness * jnp.repeat(heights, shape[axis_at] // shards_of).reshape([-1 if axis == axis_at else 1 for axis in range(len(shape))])
    return loudness


def noise(rng, shape, deviation, reach, cuts=(), kind=jnp.bfloat16):
    values = deviation * jax.random.normal(rng, shape, jnp.float32)
    if cuts:
        values = values * block_levels(rng, shape, cuts, -0.22, 0.18)
    return jnp.clip(values, -reach, reach).astype(kind)


def setup_inputs(seed: int = 0) -> dict:
    key_list = jax.random.split(jax.random.key(seed), 6)
    return {
        "records": draw_records(jax.random.fold_in(key_list[5], 71), 0),
        "band_taps": noise(key_list[1], (BT,), BT ** -0.5, 0.75, (), jnp.float32),
        "white_taps": noise(key_list[2], (WT, CHANNELS), WT ** -0.5, 1.5, ((1, 128),), jnp.float32),
        "live_mask": plant((jax.random.randint(key_list[3], (CHANNELS,), 0, 8) < 7).astype(jnp.int32), jax.random.fold_in(key_list[3], 1), 0, 1),
        "partners": draw_partners(jax.random.fold_in(key_list[5], 71), 0),
    }


def bin_numbers(samples, bin_count):
    return samples // 64 + samples // (4 * bin_count) * jnp.arange(bin_count, dtype=jnp.int32)

def rotation(products, samples):
    angles = jnp.mod(products, samples).astype(jnp.float32) * (2.0 * math.pi / samples)
    return (jnp.cos(angles), jnp.sin(angles))

def dft_table(samples, bin_index):
    sample_index = jnp.arange(samples, dtype=jnp.int32)
    cos_part, sin_part = rotation(sample_index[:, None] * bin_index[None, :], samples)
    return jnp.concatenate([cos_part, -sin_part], axis=1).astype(jnp.bfloat16)

def responses(band_taps, white_taps, bin_index, samples):
    highest = lax.Precision.HIGHEST
    band_cos, band_sin = rotation(jnp.arange(band_taps.shape[0], dtype=jnp.int32)[:, None] * bin_index[None, :], samples)
    white_cos, white_sin = rotation(jnp.arange(white_taps.shape[0], dtype=jnp.int32)[:, None] * bin_index[None, :], samples)
    band_real = jnp.dot(band_taps, band_cos, precision=highest)
    band_imag = -jnp.dot(band_taps, band_sin, precision=highest)
    white_real = jnp.dot(white_taps.T, white_cos, precision=highest)
    white_imag = -jnp.dot(white_taps.T, white_sin, precision=highest)
    resp_real = white_real * band_real[None, :] - white_imag * band_imag[None, :]
    resp_imag = white_real * band_imag[None, :] + white_imag * band_real[None, :]
    return (resp_real, resp_imag)

def filtered(raw_spec, resp_real, resp_imag, live_values):
    bin_count = resp_real.shape[1]
    spec_real = raw_spec[..., :bin_count]
    spec_imag = raw_spec[..., bin_count:]
    real_resp = resp_real[:, None, :]
    imag_resp = resp_imag[:, None, :]
    out_real = (real_resp * spec_real - imag_resp * spec_imag) * live_values[:, None, None]
    out_imag = (real_resp * spec_imag + imag_resp * spec_real) * live_values[:, None, None]
    return jnp.concatenate([out_real, out_imag], axis=2).astype(jnp.bfloat16)

def inverse_norms(flat_rows):
    values = flat_rows.astype(jnp.float32)
    mean_square = lax.optimization_barrier(jnp.sum(values * values, axis=-1)) / (SEG * NB)
    return lax.rsqrt(mean_square + 1e-06)

def turned_rows(own_block, lag_values, bin_index, samples):
    lag_cos, lag_sin = rotation(lag_values[:, None] * bin_index[None, :], samples)
    values = own_block.astype(jnp.float32).reshape(own_block.shape[0], SEG, 2, NB)
    part_real = values[:, :, 0, :][None]
    part_imag = values[:, :, 1, :][None]
    cos_factor = lag_cos[:, None, None, :]
    sin_factor = lag_sin[:, None, None, :]
    new_real = part_real * cos_factor - part_imag * sin_factor
    new_imag = part_real * sin_factor + part_imag * cos_factor
    stacked = jnp.stack([new_real, new_imag], axis=3)
    return stacked.astype(jnp.bfloat16).reshape(lag_values.shape[0] * own_block.shape[0], -1)

def tile_sums(turned, chosen, own_scale, part_scale, lag_count):
    rounds, row_count, inner_size = chosen.shape
    flat_rows = chosen.reshape(rounds * row_count, inner_size)
    tile_totals = lax.dot_general(turned, flat_rows, (((1,), (1,)), ((), ())), preferred_element_type=jnp.float32)
    tile_totals = tile_totals.reshape(lag_count, row_count, rounds, row_count)
    scaled = tile_totals * own_scale[None, :, None, None] * part_scale[None, None, :, :] * (1.0 / math.sqrt(SEG * NB))
    return jnp.transpose(scaled, (2, 0, 1, 3))

def reference(records, band_taps, white_taps, live_mask, partners):
    samples = records.shape[1]
    bin_index = bin_numbers(samples, NB)
    transform = dft_table(samples, bin_index)
    resp_real, resp_imag = responses(band_taps, white_taps, bin_index, samples)
    live_values = live_mask.astype(jnp.float32)

    def one_segment(segment_data):
        raw_spec = jnp.dot(segment_data.T, transform, preferred_element_type=jnp.float32)
        return filtered(raw_spec[:, None, :], resp_real, resp_imag, live_values)[:, 0, :]
    per_seg = lax.map(one_segment, records)
    spectra = jnp.transpose(per_seg, (1, 0, 2)).reshape(CHANNELS, SEG * 2 * NB)
    scales = inverse_norms(spectra)
    blocks = spectra.reshape(BLOCKS, CB, SEG * 2 * NB)
    block_scales = scales.reshape(BLOCKS, CB)
    lag_values = 3 * (jnp.arange(LAGS, dtype=jnp.int32) - LAGS // 2)

    def one_block(block_index):
        own_block = blocks[block_index]
        mate_index = partners[:, block_index]
        chosen = blocks[mate_index]
        turned = turned_rows(own_block, lag_values, bin_index, samples)
        return tile_sums(turned, chosen, block_scales[block_index], block_scales[mate_index], LAGS)
    all_tiles = lax.map(one_block, jnp.arange(BLOCKS, dtype=jnp.int32))
    return jnp.transpose(all_tiles, (1, 2, 0, 3, 4)).reshape(ROUNDS, LAGS, CHANNELS, CB)
```

```python
import functools
import math

import jax
import jax.numpy as jnp
import ml_dtypes
import numpy as np
from jax import lax
from jax.experimental import pallas as pl
from jax.experimental.pallas import tpu as pltpu
from jax.sharding import PartitionSpec as P

NB = 128
SEG = 6
LAGS = 32
ROUNDS = 6
CHUNK = 256


def angles(products, samples):
    return np.mod(products, samples).astype(np.float32) * np.float32(2.0 * math.pi / samples)


def tables(samples, band_count, white_count, half_lags):
    bins = (samples // 64 + samples // (4 * NB) * np.arange(NB)).astype(np.int64)
    period = samples // math.gcd(samples, int(np.gcd.reduce(bins)))
    wave = angles(bins[:, None] * np.arange(period)[None, :], samples)
    dft = np.concatenate([np.cos(wave), -np.sin(wave)], axis=0).astype(ml_dtypes.bfloat16)
    band = angles(bins[:, None] * np.arange(band_count)[None, :], samples)
    white = angles(bins[:, None] * np.arange(white_count)[None, :], samples)
    lag_values = 3 * (np.arange(LAGS) - LAGS // 2)
    lag = angles(lag_values[:, None] * bins[None, :], samples)
    lag_table = np.stack([np.cos(lag), np.sin(lag)], axis=0).astype(np.float32)
    lag_table = lag_table.reshape(2, LAGS // half_lags, half_lags, 1, NB).transpose(1, 0, 2, 3, 4)
    return (
        dft,
        np.stack([np.cos(band), -np.sin(band)]).astype(np.float32),
        np.concatenate([np.cos(white), -np.sin(white)], axis=0).astype(np.float32),
        lag_table,
    )


def spectra_kernel(
    rec_hbm, dft_hbm, band_hbm, white_hbm, band_taps, white_taps, live_hbm, out_ref,
    rec_ref, dft_ref, band_table, white_table, band_ref, white_ref, live_ref, sems, rec_sems,
):
    segments, samples, channels = rec_ref.shape
    small = [
        (band_hbm, band_table),
        (white_hbm, white_table),
        (band_taps, band_ref),
        (white_taps, white_ref),
        (live_hbm, live_ref),
        (dft_hbm, dft_ref),
    ]
    copies = [pltpu.make_async_copy(a, b, sems.at[k]) for k, (a, b) in enumerate(small)]
    loads = [
        pltpu.make_async_copy(rec_hbm.at[seg], rec_ref.at[seg], rec_sems.at[seg])
        for seg in range(segments)
    ]
    for copy in copies + loads:
        copy.start()
    for copy in copies:
        copy.wait()
    band = band_ref[...]
    band_real = jnp.sum(band_table[0] * band, axis=1, keepdims=True)
    band_imag = jnp.sum(band_table[1] * band, axis=1, keepdims=True)
    white = jnp.dot(
        white_table[...],
        white_ref[...],
        precision=lax.Precision.HIGHEST,
        preferred_element_type=jnp.float32,
    )
    white_real, white_imag = white[:NB], white[NB:]
    live = live_ref[...].astype(jnp.float32)
    resp_real = white_real * band_real - white_imag * band_imag
    resp_imag = white_real * band_imag + white_imag * band_real
    period = dft_ref.shape[1]
    for seg in range(segments):
        loads[seg].wait()
        parts = [rec_ref[seg, k * period : (k + 1) * period, :] for k in range(samples // period)]
        wide = jnp.dot(
            dft_ref[...], jnp.concatenate(parts, axis=1), preferred_element_type=jnp.float32
        )
        raw = wide[:, :channels]
        for k in range(1, len(parts)):
            raw = raw + wide[:, k * channels : (k + 1) * channels]
        raw_real, raw_imag = raw[:NB], raw[NB:]
        real = (resp_real * raw_real - resp_imag * raw_imag) * live
        imag = (resp_real * raw_imag + resp_imag * raw_real) * live
        row = seg * 2 * NB
        out_ref[row : row + NB, :] = real.astype(jnp.bfloat16)
        out_ref[row + NB : row + 2 * NB, :] = imag.astype(jnp.bfloat16)


def turn_kernel(own_ref, other_ref, lag_ref, turned_ref, scale_ref, rows_ref):
    half = own_ref.shape[0]
    channels = own_ref.shape[1]
    for index, ref in enumerate((own_ref, other_ref)):
        for k in range(0, half, NB):
            tile = ref[k : k + NB, :].astype(jnp.float32)
            rows_ref[:, index * half + k : index * half + k + NB] = tile.T
    values = rows_ref[...]
    mean_square = jnp.sum(values * values, axis=1, keepdims=True) / (SEG * NB)
    scale_ref[...] = jnp.broadcast_to(lax.rsqrt(mean_square + 1e-06), scale_ref.shape)

    def one_lag(lag, carry):
        cos_factor = lag_ref[0, lag]
        sin_factor = lag_ref[1, lag]
        start = pl.multiple_of(lag * channels, channels)
        for k in range(0, 2 * half, 2 * NB):
            real = rows_ref[:, k : k + NB]
            imag = rows_ref[:, k + NB : k + 2 * NB]
            new_real = real * cos_factor - imag * sin_factor
            new_imag = real * sin_factor + imag * cos_factor
            turned_ref[pl.ds(start, channels), k : k + NB] = new_real.astype(jnp.bfloat16)
            turned_ref[pl.ds(start, channels), k + NB : k + 2 * NB] = new_imag.astype(jnp.bfloat16)
        return carry

    lax.fori_loop(0, lag_ref.shape[1], one_lag, 0)


def column_scale(first, second):
    total = jnp.zeros((1, first.shape[1]), jnp.float32)
    for part in (first, second):
        values = part[...].astype(jnp.float32)
        total = total + jnp.sum(values * values, axis=0, keepdims=True)
    return lax.rsqrt(total / (SEG * NB) + 1e-06)


def pair_kernel(half, rows_at, slot_ref, turned_ref, scale_ref, *rest):
    out_ref, stage, sems = rest[-3:]
    channels = scale_ref.shape[0]
    ah, ao, bh, bo = [ref.at[at : at + half] for ref, at in zip(rest[:4], rows_at)]
    near = jnp.concatenate([ah[...], bh[...]], axis=1)
    far = jnp.concatenate([ao[...], bo[...]], axis=1)
    rows = turned_ref.shape[0]
    lags = CHUNK // channels
    copies = []
    for chunk in range(rows // CHUNK):
        start = chunk * CHUNK
        totals = jnp.dot(
            turned_ref[start : start + CHUNK, :half], near, preferred_element_type=jnp.float32
        ) + jnp.dot(
            turned_ref[start : start + CHUNK, half:], far, preferred_element_type=jnp.float32
        )
        if chunk == 0:
            own = scale_ref[...] * (1.0 / math.sqrt(SEG * NB))
            scales = [own * column_scale(ah, ao), own * column_scale(bh, bo)]
        for lag in range(lags):
            row = lag * channels
            for side in range(2):
                stage[side, chunk * lags + lag] = (
                    totals[row : row + channels, side * channels : (side + 1) * channels]
                    * scales[side]
                )
        for side in range(2):
            copy = pltpu.make_async_copy(
                stage.at[side, pl.ds(chunk * lags, lags)],
                out_ref.at[slot_ref[side], pl.ds(chunk * lags, lags)],
                sems.at[side, chunk],
            )
            copy.start()
            copies.append(copy)
    for copy in copies:
        copy.wait()


VMEM = pl.BlockSpec(memory_space=pltpu.VMEM)


def own_spectra(records, band_taps, white_taps, live_mask, consts):
    segments, samples, channels = records.shape
    dft, band_table, white_table = consts
    return pl.pallas_call(
        spectra_kernel,
        out_shape=jax.ShapeDtypeStruct((segments * 2 * NB, channels), jnp.bfloat16),
        in_specs=[pl.BlockSpec(memory_space=pltpu.HBM)] * 7,
        out_specs=VMEM,
        scratch_shapes=[
            pltpu.VMEM(records.shape, records.dtype),
            pltpu.VMEM(dft.shape, dft.dtype),
            pltpu.VMEM(band_table.shape, jnp.float32),
            pltpu.VMEM(white_table.shape, jnp.float32),
            pltpu.VMEM((1, band_taps.shape[0]), jnp.float32),
            pltpu.VMEM(white_taps.shape, jnp.float32),
            pltpu.VMEM((1, channels), jnp.int32),
            pltpu.SemaphoreType.DMA((6,)),
            pltpu.SemaphoreType.DMA((segments,)),
        ],
        name="spectra",
        compiler_params=pltpu.CompilerParams(vmem_limit_bytes=60 << 20),
        cost_estimate=pl.CostEstimate(
            flops=2 * segments * samples * channels * 2 * NB,
            bytes_accessed=2 * segments * samples * channels,
            transcendentals=0,
        ),
    )(
        records,
        dft,
        band_table,
        white_table,
        band_taps.reshape(1, -1),
        white_taps,
        live_mask.reshape(1, -1),
    )


def turned_rows(own, other, lag_table):
    half, channels = own.shape
    lag_count = lag_table.shape[1]
    return pl.pallas_call(
        turn_kernel,
        out_shape=(
            jax.ShapeDtypeStruct((lag_count * channels, 2 * half), jnp.bfloat16),
            jax.ShapeDtypeStruct((channels, channels), jnp.float32),
        ),
        in_specs=[VMEM] * 3,
        out_specs=(VMEM, VMEM),
        scratch_shapes=[pltpu.VMEM((channels, 2 * half), jnp.float32)],
        name="turn",
        compiler_params=pltpu.CompilerParams(vmem_limit_bytes=24 << 20),
    )(own, other, lag_table)


def pair_sums(slots, turned, scale, first, second, lag_count, previous):
    channels = scale.shape[0]
    half = turned.shape[1] // 2
    pieces = [*first, *second]
    operands = [slots, turned, scale] + [array for array, _ in pieces]
    specs = [pl.BlockSpec(memory_space=pltpu.SMEM)] + [VMEM] * 6
    aliases = {}
    if previous is not None:
        aliases = {len(operands): 0}
        operands.append(previous)
        specs.append(pl.BlockSpec(memory_space=pl.ANY))
    return pl.pallas_call(
        functools.partial(pair_kernel, half, [at for _, at in pieces]),
        out_shape=jax.ShapeDtypeStruct((ROUNDS, lag_count, channels, channels), jnp.float32),
        in_specs=specs,
        out_specs=pl.BlockSpec(memory_space=pl.ANY),
        scratch_shapes=[
            pltpu.VMEM((2, lag_count, channels, channels), jnp.float32),
            pltpu.SemaphoreType.DMA((2, lag_count * channels // CHUNK)),
        ],
        input_output_aliases=aliases,
        name="pair",
        compiler_params=pltpu.CompilerParams(vmem_limit_bytes=24 << 20),
    )(*operands)


def shifted(value, steps):
    count = lax.axis_size("chan")
    return lax.ppermute(value, "chan", [(s, (s + steps) % count) for s in range(count)])


def neighbour(value):
    return lax.ppermute(value, "chan", [(s, s ^ 1) for s in range(lax.axis_size("chan"))])


def mirrored(value):
    return lax.ppermute(value, "tm", [(0, 1), (1, 0)])


def local(consts, records, band_taps, white_taps, live_mask, partners):
    lag_count = LAGS // lax.axis_size("tm")
    my_block = lax.axis_index("chan")
    block_count = lax.axis_size("chan")
    is_odd = my_block % 2 == 1
    half = own_spectra(records, band_taps, white_taps, live_mask, consts[:3])

    delta = jnp.mod(partners[:, 0] - my_block + block_count // 2, block_count) - block_count // 2
    inner = jnp.where(is_odd, -1, 1)
    two = jnp.full_like(inner, 2)
    offsets = jnp.stack([-two, two, inner, -inner, -2 * two, 2 * two])
    rounds = jnp.arange(ROUNDS, dtype=jnp.int32)
    slots = jnp.sum(
        jnp.where(delta[None, :] == offsets[:, None], rounds[None, :], 0), axis=1
    ).astype(jnp.int32)
    lag_table = lax.dynamic_index_in_dim(consts[3], lax.axis_index("tm"), 0, keepdims=False)

    far = mirrored(half)
    low2, high2 = shifted(half, 2), shifted(half, -2)
    chip = neighbour(half)
    far, low2, high2, chip = lax.optimization_barrier((far, low2, high2, chip))
    both_far = mirrored(jnp.concatenate([low2, high2], axis=0))
    mixed = neighbour(jnp.concatenate([far, jnp.where(is_odd, low2, high2)], axis=0))
    low4, high4 = shifted(low2, 2), shifted(high2, -2)
    low4_far, high4_far = shifted(far, 4), shifted(far, -4)
    turned, scale = turned_rows(half, far, lag_table)
    size = half.shape[0]
    sent = jnp.where(is_odd, both_far[:size], both_far[size:])
    sent, turned = lax.optimization_barrier((sent, turned))
    across_far = neighbour(sent)

    near2 = ((low2, 0), (both_far, 0)), ((high2, 0), (both_far, size))
    near1 = ((chip, 0), (mixed, 0)), ((mixed, size), (across_far, 0))
    near4 = ((low4, 0), (low4_far, 0)), ((high4, 0), (high4_far, 0))
    out = pair_sums(slots[0:2], turned, scale, *near2, lag_count, None)
    out = pair_sums(slots[2:4], turned, scale, *near1, lag_count, out)
    return pair_sums(slots[4:6], turned, scale, *near4, lag_count, out)


def solution(mesh):
    def whole(records, band_taps, white_taps, live_mask, partners):
        consts = tables(
            records.shape[1], band_taps.shape[0], white_taps.shape[0], LAGS // mesh.shape["tm"]
        )
        return jax.shard_map(
            functools.partial(local, consts),
            mesh=mesh,
            in_specs=(P("tm", None, "chan"), P(), P(None, "chan"), P("chan"), P(None, "chan")),
            out_specs=P(None, "tm", "chan", None),
            check_vma=False,
        )(records, band_taps, white_taps, live_mask, partners)

    return whole
```

```python
import functools
import math

import jax
import jax.numpy as jnp
import ml_dtypes
import numpy as np
from jax import lax
from jax.experimental import pallas as pl
from jax.experimental.pallas import tpu as pltpu
from jax.sharding import PartitionSpec as P

NB = 128
SEG = 6
LAGS = 32
ROUNDS = 6
CHUNK = 256


def angles(products, samples):
    return np.mod(products, samples).astype(np.float32) * np.float32(2.0 * math.pi / samples)


def tables(samples, band_count, white_count, half_lags):
    bins = (samples // 64 + samples // (4 * NB) * np.arange(NB)).astype(np.int64)
    period = samples // math.gcd(samples, int(np.gcd.reduce(bins)))
    wave = angles(bins[:, None] * np.arange(period)[None, :], samples)
    dft = np.concatenate([np.cos(wave), -np.sin(wave)], axis=0).astype(ml_dtypes.bfloat16)
    band = angles(bins[:, None] * np.arange(band_count)[None, :], samples)
    white = angles(bins[:, None] * np.arange(white_count)[None, :], samples)
    lag_values = 3 * (np.arange(LAGS) - LAGS // 2)
    lag = angles(lag_values[:, None] * bins[None, :], samples)
    lag_table = np.stack([np.cos(lag), np.sin(lag)], axis=0).astype(np.float32)
    lag_table = lag_table.reshape(2, LAGS // half_lags, half_lags, 1, NB).transpose(1, 0, 2, 3, 4)
    taps = np.zeros((2 * NB, -(-(band_count + white_count) // 128) * 128), np.float32)
    for at, wave in ((0, band), (band_count, white)):
        taps[:, at : at + wave.shape[1]] = np.concatenate([np.cos(wave), -np.sin(wave)], axis=0)
    return dft, taps, lag_table


def spectra_kernel(
    rec_hbm, dft_hbm, table_hbm, band_taps, white_taps, live_hbm, out_ref,
    rec_ref, dft_ref, table_ref, band_ref, white_ref, live_ref, sems, rec_sems,
):
    segments, samples, channels = rec_ref.shape
    small = [
        (table_hbm, table_ref),
        (band_taps, band_ref),
        (white_taps, white_ref),
        (live_hbm, live_ref),
    ]
    copies = [pltpu.make_async_copy(a, b, sems.at[k]) for k, (a, b) in enumerate(small)]
    dft_copy = pltpu.make_async_copy(dft_hbm, dft_ref, sems.at[len(small)])
    loads = [
        pltpu.make_async_copy(rec_hbm.at[seg], rec_ref.at[seg], rec_sems.at[seg])
        for seg in range(segments)
    ]
    for copy in copies + [dft_copy] + loads:
        copy.start()
    for copy in copies:
        copy.wait()
    band_count = band_ref.shape[1]
    white_count = white_ref.shape[0]
    band_sum = jnp.sum(table_ref[:, :band_count] * band_ref[...], axis=1, keepdims=True)
    band_real, band_imag = band_sum[:NB], band_sum[NB:]
    white = jnp.dot(
        table_ref[:, band_count : band_count + white_count],
        white_ref[...],
        precision=lax.Precision.HIGHEST,
        preferred_element_type=jnp.float32,
    )
    white_real, white_imag = white[:NB], white[NB:]
    live = live_ref[...].astype(jnp.float32)
    resp_real = white_real * band_real - white_imag * band_imag
    resp_imag = white_real * band_imag + white_imag * band_real
    period = dft_ref.shape[1]
    dft_copy.wait()
    for seg in range(segments):
        loads[seg].wait()
        parts = [rec_ref[seg, k * period : (k + 1) * period, :] for k in range(samples // period)]
        wide = jnp.dot(
            dft_ref[...], jnp.concatenate(parts, axis=1), preferred_element_type=jnp.float32
        )
        raw = wide[:, :channels]
        for k in range(1, len(parts)):
            raw = raw + wide[:, k * channels : (k + 1) * channels]
        raw_real, raw_imag = raw[:NB], raw[NB:]
        real = (resp_real * raw_real - resp_imag * raw_imag) * live
        imag = (resp_real * raw_imag + resp_imag * raw_real) * live
        row = seg * 2 * NB
        out_ref[row : row + NB, :] = real.astype(jnp.bfloat16)
        out_ref[row + NB : row + 2 * NB, :] = imag.astype(jnp.bfloat16)


def turn_kernel(own_ref, other_ref, lag_ref, turned_ref, scale_ref, rows_ref):
    half = own_ref.shape[0]
    channels = own_ref.shape[1]
    for index, ref in enumerate((own_ref, other_ref)):
        for k in range(0, half, NB):
            tile = ref[k : k + NB, :].astype(jnp.float32)
            rows_ref[:, index * half + k : index * half + k + NB] = tile.T
    values = rows_ref[...]
    mean_square = jnp.sum(values * values, axis=1, keepdims=True) / (SEG * NB)
    scale_ref[...] = jnp.broadcast_to(lax.rsqrt(mean_square + 1e-06), scale_ref.shape)

    def one_lag(lag, carry):
        cos_factor = lag_ref[0, lag]
        sin_factor = lag_ref[1, lag]
        start = pl.multiple_of(lag * channels, channels)
        for k in range(0, 2 * half, 2 * NB):
            real = rows_ref[:, k : k + NB]
            imag = rows_ref[:, k + NB : k + 2 * NB]
            new_real = real * cos_factor - imag * sin_factor
            new_imag = real * sin_factor + imag * cos_factor
            turned_ref[pl.ds(start, channels), k : k + NB] = new_real.astype(jnp.bfloat16)
            turned_ref[pl.ds(start, channels), k + NB : k + 2 * NB] = new_imag.astype(jnp.bfloat16)
        return carry

    lax.fori_loop(0, lag_ref.shape[1], one_lag, 0)


def column_scale(first, second):
    total = jnp.zeros((1, first.shape[1]), jnp.float32)
    for part in (first, second):
        values = part[...].astype(jnp.float32)
        total = total + jnp.sum(values * values, axis=0, keepdims=True)
    return lax.rsqrt(total / (SEG * NB) + 1e-06)


def pair_kernel(half, rows_at, slot_ref, turned_ref, scale_ref, *rest):
    out_ref, stage, sems = rest[-3:]
    channels = scale_ref.shape[0]
    ah, ao, bh, bo = [ref.at[at : at + half] for ref, at in zip(rest[:4], rows_at)]
    near = jnp.concatenate([ah[...], bh[...]], axis=1)
    far = jnp.concatenate([ao[...], bo[...]], axis=1)
    rows = turned_ref.shape[0]
    lags = CHUNK // channels
    copies = []
    for chunk in range(rows // CHUNK):
        start = chunk * CHUNK
        totals = jnp.dot(
            turned_ref[start : start + CHUNK, :half], near, preferred_element_type=jnp.float32
        ) + jnp.dot(
            turned_ref[start : start + CHUNK, half:], far, preferred_element_type=jnp.float32
        )
        if chunk == 0:
            own = scale_ref[...] * (1.0 / math.sqrt(SEG * NB))
            scales = [own * column_scale(ah, ao), own * column_scale(bh, bo)]
        for lag in range(lags):
            row = lag * channels
            for side in range(2):
                stage[side, chunk * lags + lag] = (
                    totals[row : row + channels, side * channels : (side + 1) * channels]
                    * scales[side]
                )
        for side in range(2):
            copy = pltpu.make_async_copy(
                stage.at[side, pl.ds(chunk * lags, lags)],
                out_ref.at[slot_ref[side], pl.ds(chunk * lags, lags)],
                sems.at[side, chunk],
            )
            copy.start()
            copies.append(copy)
    for copy in copies:
        copy.wait()


VMEM = pl.BlockSpec(memory_space=pltpu.VMEM)


def own_spectra(records, band_taps, white_taps, live_mask, consts):
    segments, samples, channels = records.shape
    dft, table = consts
    return pl.pallas_call(
        spectra_kernel,
        out_shape=jax.ShapeDtypeStruct((segments * 2 * NB, channels), jnp.bfloat16),
        in_specs=[pl.BlockSpec(memory_space=pltpu.HBM)] * 6,
        out_specs=VMEM,
        scratch_shapes=[
            pltpu.VMEM(records.shape, records.dtype),
            pltpu.VMEM(dft.shape, dft.dtype),
            pltpu.VMEM(table.shape, jnp.float32),
            pltpu.VMEM((1, band_taps.shape[0]), jnp.float32),
            pltpu.VMEM(white_taps.shape, jnp.float32),
            pltpu.VMEM((1, channels), jnp.int32),
            pltpu.SemaphoreType.DMA((5,)),
            pltpu.SemaphoreType.DMA((segments,)),
        ],
        name="spectra",
        compiler_params=pltpu.CompilerParams(vmem_limit_bytes=60 << 20),
        cost_estimate=pl.CostEstimate(
            flops=2 * segments * samples * channels * 2 * NB,
            bytes_accessed=2 * segments * samples * channels,
            transcendentals=0,
        ),
    )(
        records,
        dft,
        table,
        band_taps.reshape(1, -1),
        white_taps,
        live_mask.reshape(1, -1),
    )


def turned_rows(own, other, lag_table):
    half, channels = own.shape
    lag_count = lag_table.shape[1]
    return pl.pallas_call(
        turn_kernel,
        out_shape=(
            jax.ShapeDtypeStruct((lag_count * channels, 2 * half), jnp.bfloat16),
            jax.ShapeDtypeStruct((channels, channels), jnp.float32),
        ),
        in_specs=[VMEM] * 3,
        out_specs=(VMEM, VMEM),
        scratch_shapes=[pltpu.VMEM((channels, 2 * half), jnp.float32)],
        name="turn",
        compiler_params=pltpu.CompilerParams(vmem_limit_bytes=24 << 20),
    )(own, other, lag_table)


def pair_sums(slots, turned, scale, first, second, lag_count, previous):
    channels = scale.shape[0]
    half = turned.shape[1] // 2
    pieces = [*first, *second]
    operands = [slots, turned, scale] + [array for array, _ in pieces]
    specs = [pl.BlockSpec(memory_space=pltpu.SMEM)] + [VMEM] * 6
    aliases = {}
    if previous is not None:
        aliases = {len(operands): 0}
        operands.append(previous)
        specs.append(pl.BlockSpec(memory_space=pl.ANY))
    return pl.pallas_call(
        functools.partial(pair_kernel, half, [at for _, at in pieces]),
        out_shape=jax.ShapeDtypeStruct((ROUNDS, lag_count, channels, channels), jnp.float32),
        in_specs=specs,
        out_specs=pl.BlockSpec(memory_space=pl.ANY),
        scratch_shapes=[
            pltpu.VMEM((2, lag_count, channels, channels), jnp.float32),
            pltpu.SemaphoreType.DMA((2, lag_count * channels // CHUNK)),
        ],
        input_output_aliases=aliases,
        name="pair",
        compiler_params=pltpu.CompilerParams(vmem_limit_bytes=24 << 20),
    )(*operands)


def shifted(value, steps):
    count = lax.axis_size("chan")
    return lax.ppermute(value, "chan", [(s, (s + steps) % count) for s in range(count)])


def neighbour(value):
    return lax.ppermute(value, "chan", [(s, s ^ 1) for s in range(lax.axis_size("chan"))])


def swapped(value, partner):
    count = lax.axis_size("chan")
    return lax.ppermute(value, "chan", [(s, partner(s) % count) for s in range(count)])


def first_swap(value):
    return swapped(value, lambda s: s + 2 if s // 2 % 2 == 0 else s - 2)


def second_swap(value):
    return swapped(value, lambda s: s - 2 if s // 2 % 2 == 0 else s + 2)


def first_far_swap(value):
    return swapped(value, lambda s: s + 4 if s // 4 % 2 == 0 else s - 4)


def second_far_swap(value):
    return swapped(value, lambda s: s - 4 if s // 4 % 2 == 0 else s + 4)


def mirrored(value):
    return lax.ppermute(value, "tm", [(0, 1), (1, 0)])


def local(consts, records, band_taps, white_taps, live_mask, partners):
    lag_count = LAGS // lax.axis_size("tm")
    my_block = lax.axis_index("chan")
    block_count = lax.axis_size("chan")
    is_odd = my_block % 2 == 1
    half = own_spectra(records, band_taps, white_taps, live_mask, consts[:2])

    delta = jnp.mod(partners[:, 0] - my_block + block_count // 2, block_count) - block_count // 2
    inner = jnp.where(is_odd, -1, 1)
    two = jnp.full_like(inner, 2)
    offsets = jnp.stack([-two, two, inner, -inner, -2 * two, 2 * two])
    rounds = jnp.arange(ROUNDS, dtype=jnp.int32)
    slots = jnp.sum(
        jnp.where(delta[None, :] == offsets[:, None], rounds[None, :], 0), axis=1
    ).astype(jnp.int32)
    lag_table = lax.dynamic_index_in_dim(consts[2], lax.axis_index("tm"), 0, keepdims=False)

    far = mirrored(half)
    low2, high2 = shifted(half, 2), shifted(half, -2)
    chip = neighbour(half)
    far, low2, high2, chip = lax.optimization_barrier((far, low2, high2, chip))
    both_far = mirrored(jnp.concatenate([low2, high2], axis=0))
    mixed = neighbour(jnp.concatenate([far, jnp.where(is_odd, low2, high2)], axis=0))
    low4, high4 = shifted(low2, 2), shifted(high2, -2)
    low4_far, high4_far = shifted(far, 4), shifted(far, -4)
    turned, scale = turned_rows(half, far, lag_table)
    size = half.shape[0]
    sent = jnp.where(is_odd, both_far[:size], both_far[size:])
    sent, turned = lax.optimization_barrier((sent, turned))
    across_far = neighbour(sent)

    near2 = ((low2, 0), (both_far, 0)), ((high2, 0), (both_far, size))
    near1 = ((chip, 0), (mixed, 0)), ((mixed, size), (across_far, 0))
    near4 = ((low4, 0), (low4_far, 0)), ((high4, 0), (high4_far, 0))
    out = pair_sums(slots[0:2], turned, scale, *near2, lag_count, None)
    out = pair_sums(slots[2:4], turned, scale, *near1, lag_count, out)
    return pair_sums(slots[4:6], turned, scale, *near4, lag_count, out)


def solution(mesh):
    def whole(records, band_taps, white_taps, live_mask, partners):
        consts = tables(
            records.shape[1], band_taps.shape[0], white_taps.shape[0], LAGS // mesh.shape["tm"]
        )
        return jax.shard_map(
            functools.partial(local, consts),
            mesh=mesh,
            in_specs=(P("tm", None, "chan"), P(), P(None, "chan"), P("chan"), P(None, "chan")),
            out_specs=P(None, "tm", "chan", None),
            check_vma=False,
        )(records, band_taps, white_taps, live_mask, partners)

    return whole
```

```python
import functools
import math

import jax
import jax.numpy as jnp
import ml_dtypes
import numpy as np
from jax import lax
from jax.experimental import pallas as pl
from jax.experimental.pallas import tpu as pltpu
from jax.sharding import PartitionSpec as P

NB = 128
SEG = 6
LAGS = 32
ROUNDS = 6
CHUNK = 256


def angles(products, samples):
    return np.mod(products, samples).astype(np.float32) * np.float32(2.0 * math.pi / samples)


def tables(samples, band_count, white_count, half_lags):
    bins = (samples // 64 + samples // (4 * NB) * np.arange(NB)).astype(np.int64)
    period = samples // math.gcd(samples, int(np.gcd.reduce(bins)))
    wave = angles(bins[:, None] * np.arange(period)[None, :], samples)
    dft = np.concatenate([np.cos(wave), -np.sin(wave)], axis=0).astype(ml_dtypes.bfloat16)
    band = angles(bins[:, None] * np.arange(band_count)[None, :], samples)
    white = angles(bins[:, None] * np.arange(white_count)[None, :], samples)
    lag_values = 3 * (np.arange(LAGS) - LAGS // 2)
    lag = angles(lag_values[:, None] * bins[None, :], samples)
    lag_table = np.stack([np.cos(lag), np.sin(lag)], axis=0).astype(np.float32)
    lag_table = lag_table.reshape(2, LAGS // half_lags, half_lags, 1, NB).transpose(1, 0, 2, 3, 4)
    taps = np.zeros((2 * NB, -(-(band_count + white_count) // 128) * 128), np.float32)
    for at, wave in ((0, band), (band_count, white)):
        taps[:, at : at + wave.shape[1]] = np.concatenate([np.cos(wave), -np.sin(wave)], axis=0)
    return dft, taps, lag_table


def spectra_kernel(
    rec_hbm, dft_hbm, table_hbm, band_taps, white_taps, live_hbm, out_ref,
    rec_ref, dft_ref, table_ref, band_ref, white_ref, live_ref, sems, rec_sems,
):
    segments, samples, channels = rec_ref.shape
    small = [
        (table_hbm, table_ref),
        (band_taps, band_ref),
        (white_taps, white_ref),
        (live_hbm, live_ref),
    ]
    copies = [pltpu.make_async_copy(a, b, sems.at[k]) for k, (a, b) in enumerate(small)]
    dft_copy = pltpu.make_async_copy(dft_hbm, dft_ref, sems.at[len(small)])
    loads = [
        pltpu.make_async_copy(rec_hbm.at[seg], rec_ref.at[seg], rec_sems.at[seg])
        for seg in range(segments)
    ]
    for copy in copies + [dft_copy] + loads:
        copy.start()
    for copy in copies:
        copy.wait()
    band_count = band_ref.shape[1]
    white_count = white_ref.shape[0]
    band_sum = jnp.sum(table_ref[:, :band_count] * band_ref[...], axis=1, keepdims=True)
    band_real, band_imag = band_sum[:NB], band_sum[NB:]
    white = jnp.dot(
        table_ref[:, band_count : band_count + white_count],
        white_ref[...],
        precision=lax.Precision.HIGHEST,
        preferred_element_type=jnp.float32,
    )
    white_real, white_imag = white[:NB], white[NB:]
    live = live_ref[...].astype(jnp.float32)
    resp_real = white_real * band_real - white_imag * band_imag
    resp_imag = white_real * band_imag + white_imag * band_real
    period = dft_ref.shape[1]
    dft_copy.wait()
    for seg in range(segments):
        loads[seg].wait()
        parts = [rec_ref[seg, k * period : (k + 1) * period, :] for k in range(samples // period)]
        wide = jnp.dot(
            dft_ref[...], jnp.concatenate(parts, axis=1), preferred_element_type=jnp.float32
        )
        raw = wide[:, :channels]
        for k in range(1, len(parts)):
            raw = raw + wide[:, k * channels : (k + 1) * channels]
        raw_real, raw_imag = raw[:NB], raw[NB:]
        real = (resp_real * raw_real - resp_imag * raw_imag) * live
        imag = (resp_real * raw_imag + resp_imag * raw_real) * live
        row = seg * 2 * NB
        out_ref[row : row + NB, :] = real.astype(jnp.bfloat16)
        out_ref[row + NB : row + 2 * NB, :] = imag.astype(jnp.bfloat16)


def turn_kernel(own_ref, other_ref, lag_ref, turned_ref, scale_ref, rows_ref):
    half = own_ref.shape[0]
    channels = own_ref.shape[1]
    for index, ref in enumerate((own_ref, other_ref)):
        for k in range(0, half, NB):
            tile = ref[k : k + NB, :].astype(jnp.float32)
            rows_ref[:, index * half + k : index * half + k + NB] = tile.T
    values = rows_ref[...]
    mean_square = jnp.sum(values * values, axis=1, keepdims=True) / (SEG * NB)
    scale_ref[...] = jnp.broadcast_to(lax.rsqrt(mean_square + 1e-06), scale_ref.shape)

    def one_lag(lag, carry):
        cos_factor = lag_ref[0, lag]
        sin_factor = lag_ref[1, lag]
        start = pl.multiple_of(lag * channels, channels)
        for k in range(0, 2 * half, 2 * NB):
            real = rows_ref[:, k : k + NB]
            imag = rows_ref[:, k + NB : k + 2 * NB]
            new_real = real * cos_factor - imag * sin_factor
            new_imag = real * sin_factor + imag * cos_factor
            turned_ref[pl.ds(start, channels), k : k + NB] = new_real.astype(jnp.bfloat16)
            turned_ref[pl.ds(start, channels), k + NB : k + 2 * NB] = new_imag.astype(jnp.bfloat16)
        return carry

    lax.fori_loop(0, lag_ref.shape[1], one_lag, 0)


def column_scale(first, second):
    total = jnp.zeros((1, first.shape[1]), jnp.float32)
    for part in (first, second):
        values = part[...].astype(jnp.float32)
        total = total + jnp.sum(values * values, axis=0, keepdims=True)
    return lax.rsqrt(total / (SEG * NB) + 1e-06)


def near_kernel(half, rows_at, turned_ref, a_ref, b_ref, out_ref):
    ah, bh = [ref[at : at + half, :] for ref, at in zip((a_ref, b_ref), rows_at)]
    near = jnp.concatenate([ah, bh], axis=1)
    for start in range(0, turned_ref.shape[0], CHUNK):
        out_ref[start : start + CHUNK, :] = jnp.dot(
            turned_ref[start : start + CHUNK, :half], near, preferred_element_type=jnp.float32
        )


def pair_kernel(half, rows_at, started, slot_ref, turned_ref, scale_ref, *rest):
    out_ref, stage, sems = rest[-3:]
    channels = scale_ref.shape[0]
    ah, ao, bh, bo = [ref.at[at : at + half] for ref, at in zip(rest[:4], rows_at)]
    near = jnp.concatenate([ah[...], bh[...]], axis=1)
    far = jnp.concatenate([ao[...], bo[...]], axis=1)
    rows = turned_ref.shape[0]
    lags = CHUNK // channels
    copies = []
    for chunk in range(rows // CHUNK):
        start = chunk * CHUNK
        if started:
            totals = rest[4][start : start + CHUNK, :]
        else:
            totals = jnp.dot(
                turned_ref[start : start + CHUNK, :half], near, preferred_element_type=jnp.float32
            )
        totals = totals + jnp.dot(
            turned_ref[start : start + CHUNK, half:], far, preferred_element_type=jnp.float32
        )
        if chunk == 0:
            own = scale_ref[...] * (1.0 / math.sqrt(SEG * NB))
            scales = [own * column_scale(ah, ao), own * column_scale(bh, bo)]
        for lag in range(lags):
            row = lag * channels
            for side in range(2):
                stage[side, chunk * lags + lag] = (
                    totals[row : row + channels, side * channels : (side + 1) * channels]
                    * scales[side]
                )
        for side in range(2):
            copy = pltpu.make_async_copy(
                stage.at[side, pl.ds(chunk * lags, lags)],
                out_ref.at[slot_ref[side], pl.ds(chunk * lags, lags)],
                sems.at[side, chunk],
            )
            copy.start()
            copies.append(copy)
    for copy in copies:
        copy.wait()


VMEM = pl.BlockSpec(memory_space=pltpu.VMEM)


def own_spectra(records, band_taps, white_taps, live_mask, consts):
    segments, samples, channels = records.shape
    dft, table = consts
    return pl.pallas_call(
        spectra_kernel,
        out_shape=jax.ShapeDtypeStruct((segments * 2 * NB, channels), jnp.bfloat16),
        in_specs=[pl.BlockSpec(memory_space=pltpu.HBM)] * 6,
        out_specs=VMEM,
        scratch_shapes=[
            pltpu.VMEM(records.shape, records.dtype),
            pltpu.VMEM(dft.shape, dft.dtype),
            pltpu.VMEM(table.shape, jnp.float32),
            pltpu.VMEM((1, band_taps.shape[0]), jnp.float32),
            pltpu.VMEM(white_taps.shape, jnp.float32),
            pltpu.VMEM((1, channels), jnp.int32),
            pltpu.SemaphoreType.DMA((5,)),
            pltpu.SemaphoreType.DMA((segments,)),
        ],
        name="spectra",
        compiler_params=pltpu.CompilerParams(vmem_limit_bytes=60 << 20),
        cost_estimate=pl.CostEstimate(
            flops=2 * segments * samples * channels * 2 * NB,
            bytes_accessed=2 * segments * samples * channels,
            transcendentals=0,
        ),
    )(
        records,
        dft,
        table,
        band_taps.reshape(1, -1),
        white_taps,
        live_mask.reshape(1, -1),
    )


def turned_rows(own, other, lag_table):
    half, channels = own.shape
    lag_count = lag_table.shape[1]
    return pl.pallas_call(
        turn_kernel,
        out_shape=(
            jax.ShapeDtypeStruct((lag_count * channels, 2 * half), jnp.bfloat16),
            jax.ShapeDtypeStruct((channels, channels), jnp.float32),
        ),
        in_specs=[VMEM] * 3,
        out_specs=(VMEM, VMEM),
        scratch_shapes=[pltpu.VMEM((channels, 2 * half), jnp.float32)],
        name="turn",
        compiler_params=pltpu.CompilerParams(vmem_limit_bytes=24 << 20),
    )(own, other, lag_table)


def near_sums(turned, first, second):
    half = turned.shape[1] // 2
    (a, a_at), (b, b_at) = first, second
    return pl.pallas_call(
        functools.partial(near_kernel, half, (a_at, b_at)),
        out_shape=jax.ShapeDtypeStruct((turned.shape[0], 2 * a.shape[1]), jnp.float32),
        in_specs=[VMEM] * 3,
        out_specs=VMEM,
        name="near",
        compiler_params=pltpu.CompilerParams(vmem_limit_bytes=24 << 20),
    )(turned, a, b)


def pair_sums(slots, turned, scale, first, second, lag_count, previous, partial=None):
    channels = scale.shape[0]
    half = turned.shape[1] // 2
    pieces = [*first, *second]
    operands = [slots, turned, scale] + [array for array, _ in pieces]
    if partial is not None:
        operands.append(partial)
    specs = [pl.BlockSpec(memory_space=pltpu.SMEM)] + [VMEM] * (len(operands) - 1)
    aliases = {}
    if previous is not None:
        aliases = {len(operands): 0}
        operands.append(previous)
        specs.append(pl.BlockSpec(memory_space=pl.ANY))
    return pl.pallas_call(
        functools.partial(pair_kernel, half, [at for _, at in pieces], partial is not None),
        out_shape=jax.ShapeDtypeStruct((ROUNDS, lag_count, channels, channels), jnp.float32),
        in_specs=specs,
        out_specs=pl.BlockSpec(memory_space=pl.ANY),
        scratch_shapes=[
            pltpu.VMEM((2, lag_count, channels, channels), jnp.float32),
            pltpu.SemaphoreType.DMA((2, lag_count * channels // CHUNK)),
        ],
        input_output_aliases=aliases,
        name="pair",
        compiler_params=pltpu.CompilerParams(vmem_limit_bytes=24 << 20),
    )(*operands)


def shifted(value, steps):
    count = lax.axis_size("chan")
    return lax.ppermute(value, "chan", [(s, (s + steps) % count) for s in range(count)])


def neighbour(value):
    return lax.ppermute(value, "chan", [(s, s ^ 1) for s in range(lax.axis_size("chan"))])


def swapped(value, partner):
    count = lax.axis_size("chan")
    return lax.ppermute(value, "chan", [(s, partner(s) % count) for s in range(count)])


def first_swap(value):
    return swapped(value, lambda s: s + 2 if s // 2 % 2 == 0 else s - 2)


def second_swap(value):
    return swapped(value, lambda s: s - 2 if s // 2 % 2 == 0 else s + 2)


def first_far_swap(value):
    return swapped(value, lambda s: s + 4 if s // 4 % 2 == 0 else s - 4)


def second_far_swap(value):
    return swapped(value, lambda s: s - 4 if s // 4 % 2 == 0 else s + 4)


def mirrored(value):
    return lax.ppermute(value, "tm", [(0, 1), (1, 0)])


def local(consts, records, band_taps, white_taps, live_mask, partners):
    lag_count = LAGS // lax.axis_size("tm")
    my_block = lax.axis_index("chan")
    block_count = lax.axis_size("chan")
    is_odd = my_block % 2 == 1
    half = own_spectra(records, band_taps, white_taps, live_mask, consts[:2])

    delta = jnp.mod(partners[:, 0] - my_block + block_count // 2, block_count) - block_count // 2
    inner = jnp.where(is_odd, -1, 1)
    two = jnp.full_like(inner, 2)
    offsets = jnp.stack([-two, two, inner, -inner, -2 * two, 2 * two])
    rounds = jnp.arange(ROUNDS, dtype=jnp.int32)
    slots = jnp.sum(
        jnp.where(delta[None, :] == offsets[:, None], rounds[None, :], 0), axis=1
    ).astype(jnp.int32)
    lag_table = lax.dynamic_index_in_dim(consts[2], lax.axis_index("tm"), 0, keepdims=False)

    far = mirrored(half)
    low2, high2 = shifted(half, 2), shifted(half, -2)
    chip = neighbour(half)
    far, low2, high2, chip = lax.optimization_barrier((far, low2, high2, chip))
    both_far = mirrored(jnp.concatenate([low2, high2], axis=0))
    mixed = neighbour(jnp.concatenate([far, jnp.where(is_odd, low2, high2)], axis=0))
    low4, high4 = shifted(low2, 2), shifted(high2, -2)
    low4_far, high4_far = shifted(far, 4), shifted(far, -4)
    turned, scale = turned_rows(half, far, lag_table)
    size = half.shape[0]
    sent = jnp.where(is_odd, both_far[:size], both_far[size:])
    part2 = near_sums(turned, (low2, 0), (high2, 0))
    sent, turned, part2 = lax.optimization_barrier((sent, turned, part2))
    across_far = neighbour(sent)

    near2 = ((low2, 0), (both_far, 0)), ((high2, 0), (both_far, size))
    near1 = ((chip, 0), (mixed, 0)), ((mixed, size), (across_far, 0))
    near4 = ((low4, 0), (low4_far, 0)), ((high4, 0), (high4_far, 0))
    out = pair_sums(slots[0:2], turned, scale, *near2, lag_count, None, part2)
    out = pair_sums(slots[2:4], turned, scale, *near1, lag_count, out)
    return pair_sums(slots[4:6], turned, scale, *near4, lag_count, out)


def solution(mesh):
    def whole(records, band_taps, white_taps, live_mask, partners):
        consts = tables(
            records.shape[1], band_taps.shape[0], white_taps.shape[0], LAGS // mesh.shape["tm"]
        )
        return jax.shard_map(
            functools.partial(local, consts),
            mesh=mesh,
            in_specs=(P("tm", None, "chan"), P(), P(None, "chan"), P("chan"), P(None, "chan")),
            out_specs=P(None, "tm", "chan", None),
            check_vma=False,
        )(records, band_taps, white_taps, live_mask, partners)

    return whole
```

```python
import functools
import math

import jax
import jax.numpy as jnp
import ml_dtypes
import numpy as np
from jax import lax
from jax.experimental import pallas as pl
from jax.experimental.pallas import tpu as pltpu
from jax.sharding import PartitionSpec as P

NB = 128
SEG = 6
LAGS = 32
ROUNDS = 6
CHUNK = 256


def angles(products, samples):
    return np.mod(products, samples).astype(np.float32) * np.float32(2.0 * math.pi / samples)


def tables(samples, band_count, white_count, half_lags):
    bins = (samples // 64 + samples // (4 * NB) * np.arange(NB)).astype(np.int64)
    period = samples // math.gcd(samples, int(np.gcd.reduce(bins)))
    wave = angles(bins[:, None] * np.arange(period)[None, :], samples)
    dft = np.concatenate([np.cos(wave), -np.sin(wave)], axis=0).astype(ml_dtypes.bfloat16)
    band = angles(bins[:, None] * np.arange(band_count)[None, :], samples)
    white = angles(bins[:, None] * np.arange(white_count)[None, :], samples)
    lag_values = 3 * (np.arange(LAGS) - LAGS // 2)
    lag = angles(lag_values[:, None] * bins[None, :], samples)
    lag_table = np.stack([np.cos(lag), np.sin(lag)], axis=0).astype(np.float32)
    lag_table = lag_table.reshape(2, LAGS // half_lags, half_lags, 1, NB).transpose(1, 0, 2, 3, 4)
    taps = np.zeros((2 * NB, -(-(band_count + white_count) // 128) * 128), np.float32)
    for at, wave in ((0, band), (band_count, white)):
        taps[:, at : at + wave.shape[1]] = np.concatenate([np.cos(wave), -np.sin(wave)], axis=0)
    return dft, taps, lag_table


def spectra_kernel(
    rec_hbm, dft_hbm, table_hbm, band_taps, white_taps, live_hbm, out_ref,
    rec_ref, dft_ref, table_ref, band_ref, white_ref, live_ref, sems, rec_sems,
):
    segments, samples, channels = rec_ref.shape
    small = [
        (table_hbm, table_ref),
        (band_taps, band_ref),
        (white_taps, white_ref),
        (live_hbm, live_ref),
    ]
    copies = [pltpu.make_async_copy(a, b, sems.at[k]) for k, (a, b) in enumerate(small)]
    dft_copy = pltpu.make_async_copy(dft_hbm, dft_ref, sems.at[len(small)])
    loads = [
        pltpu.make_async_copy(rec_hbm.at[seg], rec_ref.at[seg], rec_sems.at[seg])
        for seg in range(segments)
    ]
    for copy in loads[:1] + copies + [dft_copy] + loads[1:]:
        copy.start()
    for copy in copies:
        copy.wait()
    band_count = band_ref.shape[1]
    white_count = white_ref.shape[0]
    band_sum = jnp.sum(table_ref[:, :band_count] * band_ref[...], axis=1, keepdims=True)
    band_real, band_imag = band_sum[:NB], band_sum[NB:]
    white = jnp.dot(
        table_ref[:, band_count : band_count + white_count],
        white_ref[...],
        precision=lax.Precision.HIGHEST,
        preferred_element_type=jnp.float32,
    )
    white_real, white_imag = white[:NB], white[NB:]
    live = live_ref[...].astype(jnp.float32)
    resp_real = white_real * band_real - white_imag * band_imag
    resp_imag = white_real * band_imag + white_imag * band_real
    period = dft_ref.shape[1]
    dft_copy.wait()
    for seg in range(segments):
        loads[seg].wait()
        parts = [rec_ref[seg, k * period : (k + 1) * period, :] for k in range(samples // period)]
        wide = jnp.dot(
            dft_ref[...], jnp.concatenate(parts, axis=1), preferred_element_type=jnp.float32
        )
        raw = wide[:, :channels]
        for k in range(1, len(parts)):
            raw = raw + wide[:, k * channels : (k + 1) * channels]
        raw_real, raw_imag = raw[:NB], raw[NB:]
        real = (resp_real * raw_real - resp_imag * raw_imag) * live
        imag = (resp_real * raw_imag + resp_imag * raw_real) * live
        row = seg * 2 * NB
        out_ref[row : row + NB, :] = real.astype(jnp.bfloat16)
        out_ref[row + NB : row + 2 * NB, :] = imag.astype(jnp.bfloat16)


def turn_kernel(own_ref, other_ref, lag_ref, turned_ref, scale_ref, rows_ref):
    half = own_ref.shape[0]
    channels = own_ref.shape[1]
    for index, ref in enumerate((own_ref, other_ref)):
        for k in range(0, half, NB):
            tile = ref[k : k + NB, :].astype(jnp.float32)
            rows_ref[:, index * half + k : index * half + k + NB] = tile.T
    values = rows_ref[...]
    mean_square = jnp.sum(values * values, axis=1, keepdims=True) / (SEG * NB)
    scale_ref[...] = jnp.broadcast_to(lax.rsqrt(mean_square + 1e-06), scale_ref.shape)

    def one_lag(lag, carry):
        cos_factor = lag_ref[0, lag]
        sin_factor = lag_ref[1, lag]
        start = pl.multiple_of(lag * channels, channels)
        for k in range(0, 2 * half, 2 * NB):
            real = rows_ref[:, k : k + NB]
            imag = rows_ref[:, k + NB : k + 2 * NB]
            new_real = real * cos_factor - imag * sin_factor
            new_imag = real * sin_factor + imag * cos_factor
            turned_ref[pl.ds(start, channels), k : k + NB] = new_real.astype(jnp.bfloat16)
            turned_ref[pl.ds(start, channels), k + NB : k + 2 * NB] = new_imag.astype(jnp.bfloat16)
        return carry

    lax.fori_loop(0, lag_ref.shape[1], one_lag, 0)


def column_scale(first, second):
    total = jnp.zeros((1, first.shape[1]), jnp.float32)
    for part in (first, second):
        values = part[...].astype(jnp.float32)
        total = total + jnp.sum(values * values, axis=0, keepdims=True)
    return lax.rsqrt(total / (SEG * NB) + 1e-06)


def pair_kernel(half, rows_at, slot_ref, turned_ref, scale_ref, *rest):
    out_ref, stage, sems = rest[-3:]
    channels = scale_ref.shape[0]
    ah, ao, bh, bo = [ref.at[at : at + half] for ref, at in zip(rest[:4], rows_at)]
    near = jnp.concatenate([ah[...], bh[...]], axis=1)
    far = jnp.concatenate([ao[...], bo[...]], axis=1)
    rows = turned_ref.shape[0]
    lags = CHUNK // channels
    copies = []
    for chunk in range(rows // CHUNK):
        start = chunk * CHUNK
        totals = jnp.dot(
            turned_ref[start : start + CHUNK, :half], near, preferred_element_type=jnp.float32
        ) + jnp.dot(
            turned_ref[start : start + CHUNK, half:], far, preferred_element_type=jnp.float32
        )
        if chunk == 0:
            own = scale_ref[...] * (1.0 / math.sqrt(SEG * NB))
            scales = [own * column_scale(ah, ao), own * column_scale(bh, bo)]
        for lag in range(lags):
            row = lag * channels
            for side in range(2):
                stage[side, chunk * lags + lag] = (
                    totals[row : row + channels, side * channels : (side + 1) * channels]
                    * scales[side]
                )
        for side in range(2):
            copy = pltpu.make_async_copy(
                stage.at[side, pl.ds(chunk * lags, lags)],
                out_ref.at[slot_ref[side], pl.ds(chunk * lags, lags)],
                sems.at[side, chunk],
            )
            copy.start()
            copies.append(copy)
    for copy in copies:
        copy.wait()


VMEM = pl.BlockSpec(memory_space=pltpu.VMEM)


def own_spectra(records, band_taps, white_taps, live_mask, consts):
    segments, samples, channels = records.shape
    dft, table = consts
    return pl.pallas_call(
        spectra_kernel,
        out_shape=jax.ShapeDtypeStruct((segments * 2 * NB, channels), jnp.bfloat16),
        in_specs=[pl.BlockSpec(memory_space=pltpu.HBM)] * 6,
        out_specs=VMEM,
        scratch_shapes=[
            pltpu.VMEM(records.shape, records.dtype),
            pltpu.VMEM(dft.shape, dft.dtype),
            pltpu.VMEM(table.shape, jnp.float32),
            pltpu.VMEM((1, band_taps.shape[0]), jnp.float32),
            pltpu.VMEM(white_taps.shape, jnp.float32),
            pltpu.VMEM((1, channels), jnp.int32),
            pltpu.SemaphoreType.DMA((5,)),
            pltpu.SemaphoreType.DMA((segments,)),
        ],
        name="spectra",
        compiler_params=pltpu.CompilerParams(vmem_limit_bytes=60 << 20),
        cost_estimate=pl.CostEstimate(
            flops=2 * segments * samples * channels * 2 * NB,
            bytes_accessed=2 * segments * samples * channels,
            transcendentals=0,
        ),
    )(
        records,
        dft,
        table,
        band_taps.reshape(1, -1),
        white_taps,
        live_mask.reshape(1, -1),
    )


def turned_rows(own, other, lag_table):
    half, channels = own.shape
    lag_count = lag_table.shape[1]
    return pl.pallas_call(
        turn_kernel,
        out_shape=(
            jax.ShapeDtypeStruct((lag_count * channels, 2 * half), jnp.bfloat16),
            jax.ShapeDtypeStruct((channels, channels), jnp.float32),
        ),
        in_specs=[VMEM] * 3,
        out_specs=(VMEM, VMEM),
        scratch_shapes=[pltpu.VMEM((channels, 2 * half), jnp.float32)],
        name="turn",
        compiler_params=pltpu.CompilerParams(vmem_limit_bytes=24 << 20),
    )(own, other, lag_table)


def pair_sums(slots, turned, scale, first, second, lag_count, previous):
    channels = scale.shape[0]
    half = turned.shape[1] // 2
    pieces = [*first, *second]
    operands = [slots, turned, scale] + [array for array, _ in pieces]
    specs = [pl.BlockSpec(memory_space=pltpu.SMEM)] + [VMEM] * 6
    aliases = {}
    if previous is not None:
        aliases = {len(operands): 0}
        operands.append(previous)
        specs.append(pl.BlockSpec(memory_space=pl.ANY))
    return pl.pallas_call(
        functools.partial(pair_kernel, half, [at for _, at in pieces]),
        out_shape=jax.ShapeDtypeStruct((ROUNDS, lag_count, channels, channels), jnp.float32),
        in_specs=specs,
        out_specs=pl.BlockSpec(memory_space=pl.ANY),
        scratch_shapes=[
            pltpu.VMEM((2, lag_count, channels, channels), jnp.float32),
            pltpu.SemaphoreType.DMA((2, lag_count * channels // CHUNK)),
        ],
        input_output_aliases=aliases,
        name="pair",
        compiler_params=pltpu.CompilerParams(vmem_limit_bytes=24 << 20),
    )(*operands)


def shifted(value, steps):
    count = lax.axis_size("chan")
    return lax.ppermute(value, "chan", [(s, (s + steps) % count) for s in range(count)])


def neighbour(value):
    return lax.ppermute(value, "chan", [(s, s ^ 1) for s in range(lax.axis_size("chan"))])


def swapped(value, partner):
    count = lax.axis_size("chan")
    return lax.ppermute(value, "chan", [(s, partner(s) % count) for s in range(count)])


def first_swap(value):
    return swapped(value, lambda s: s + 2 if s // 2 % 2 == 0 else s - 2)


def second_swap(value):
    return swapped(value, lambda s: s - 2 if s // 2 % 2 == 0 else s + 2)


def first_far_swap(value):
    return swapped(value, lambda s: s + 4 if s // 4 % 2 == 0 else s - 4)


def second_far_swap(value):
    return swapped(value, lambda s: s - 4 if s // 4 % 2 == 0 else s + 4)


def mirrored(value):
    return lax.ppermute(value, "tm", [(0, 1), (1, 0)])


def local(consts, records, band_taps, white_taps, live_mask, partners):
    lag_count = LAGS // lax.axis_size("tm")
    my_block = lax.axis_index("chan")
    block_count = lax.axis_size("chan")
    is_odd = my_block % 2 == 1
    half = own_spectra(records, band_taps, white_taps, live_mask, consts[:2])

    delta = jnp.mod(partners[:, 0] - my_block + block_count // 2, block_count) - block_count // 2
    inner = jnp.where(is_odd, -1, 1)
    two = jnp.full_like(inner, 2)
    offsets = jnp.stack([-two, two, inner, -inner, -2 * two, 2 * two])
    rounds = jnp.arange(ROUNDS, dtype=jnp.int32)
    slots = jnp.sum(
        jnp.where(delta[None, :] == offsets[:, None], rounds[None, :], 0), axis=1
    ).astype(jnp.int32)
    lag_table = lax.dynamic_index_in_dim(consts[2], lax.axis_index("tm"), 0, keepdims=False)

    far = mirrored(half)
    low2, high2 = shifted(half, 2), shifted(half, -2)
    chip = neighbour(half)
    far, low2, high2, chip = lax.optimization_barrier((far, low2, high2, chip))
    both_far = mirrored(jnp.concatenate([low2, high2], axis=0))
    mixed = neighbour(jnp.concatenate([far, jnp.where(is_odd, low2, high2)], axis=0))
    low4, high4 = shifted(low2, 2), shifted(high2, -2)
    low4_far, high4_far = shifted(far, 4), shifted(far, -4)
    turned, scale = turned_rows(half, far, lag_table)
    size = half.shape[0]
    sent = jnp.where(is_odd, both_far[:size], both_far[size:])
    sent, turned = lax.optimization_barrier((sent, turned))
    across_far = neighbour(sent)

    near2 = ((low2, 0), (both_far, 0)), ((high2, 0), (both_far, size))
    near1 = ((chip, 0), (mixed, 0)), ((mixed, size), (across_far, 0))
    near4 = ((low4, 0), (low4_far, 0)), ((high4, 0), (high4_far, 0))
    out = pair_sums(slots[0:2], turned, scale, *near2, lag_count, None)
    out = pair_sums(slots[2:4], turned, scale, *near1, lag_count, out)
    return pair_sums(slots[4:6], turned, scale, *near4, lag_count, out)


def solution(mesh):
    def whole(records, band_taps, white_taps, live_mask, partners):
        consts = tables(
            records.shape[1], band_taps.shape[0], white_taps.shape[0], LAGS // mesh.shape["tm"]
        )
        return jax.shard_map(
            functools.partial(local, consts),
            mesh=mesh,
            in_specs=(P("tm", None, "chan"), P(), P(None, "chan"), P("chan"), P(None, "chan")),
            out_specs=P(None, "tm", "chan", None),
            check_vma=False,
        )(records, band_taps, white_taps, live_mask, partners)

    return whole
```
